32 devices in a mesh: mom: 4 (over z), en: 2 (over y), atom: 4 (over x, core).
Axes of the slice: x: 2, y: 2, z: 4, core: 2. Of those that a mesh axis runs over, the one named last changes fastest.
Arguments:
- green_blocks: bfloat16 [16, 12, 16, 2, 128, 128], P('mom', 'en', 'atom'), may hold values from -6 to 6
- coupling: bfloat16 [4, 16, 4, 128, 128], P(None, 'atom'), may hold values from -0.25 to 0.25
- neighbours: int32 [16, 4], P('atom'), may hold values from 0 to 15, as said below
- momentum_shift: int32 [4], replicated, may hold values from -2 to 2, as said below
- energy_offset: int32 [4], replicated, may hold values from 1 to 2, as said below
- phonon_weight: float32 [4], replicated, may hold values from 0.3 to 1.5
Outputs:
- self_energy: float32 [16, 12, 16, 2, 128, 128], P('mom', 'en', 'atom')
The draws below stay inside these ranges and needn't reach their ends.
Inputs may be any that keep to these rules, and one draw needn't show every extreme that they name: `neighbours`: cluster a is bonded to (a + 2) mod 16 and (a - 2) mod 16; each other bond is to (a + d) mod 16 with d between -2 and 2. `momentum_shift`: the transfers 2 and -2 both occur. `energy_offset`: the offsets 1 and 2 both occur.
All inputs are finite; a program needn't handle non-finite values.
Results may differ from the reference program's by a relative error of at most 0.0029.
Values may be sent and summed in bfloat16 or wider, within the bound.
A program may use at most 192 MiB of HBM per device.

```python
import math
import jax
import jax.numpy as jnp
from jax import lax

O = 128
NB = 4
NQ = 4
NW = 4
REACH = 2
OFFMAX = 2
NK = 16
NE = 12
NC = 16


def draw_neighbours(key, part):
    first_key, second_key = jax.random.split(jax.random.fold_in(key, 7))
    offsets_drawn = jax.random.randint(first_key, (NC, NB), -REACH, REACH + 1)
    direction = jax.random.randint(second_key, (NC,), 0, 2) * 2 - 1
    offsets_drawn = offsets_drawn.at[:, 0].set(REACH * direction).at[:, 1].set(-REACH * direction)
    return ((jnp.arange(NC, dtype=jnp.int32)[:, None] + offsets_drawn) % NC).astype(jnp.int32)


def draw_momentum_shift(key, part):
    chooser, values_key = jax.random.split(jax.random.fold_in(key, 13))
    values = jax.random.randint(values_key, (NQ,), -REACH, REACH + 1)
    placing = jax.random.permutation(chooser, NQ)
    values = values.at[placing[0]].set(REACH).at[placing[1]].set(-REACH)
    return values.astype(jnp.int32)


def draw_energy_offset(key, part):
    chooser, values_key = jax.random.split(jax.random.fold_in(key, 17))
    values = jax.random.randint(values_key, (NW,), 1, OFFMAX + 1)
    placing = jax.random.permutation(chooser, NW)
    values = values.at[placing[0]].set(1).at[placing[1]].set(OFFMAX)
    return values.astype(jnp.int32)


def block_levels(stream_key, dims, cuts, low, high):
    loudness = 1.0
    for position, shards_of in cuts:
        heights = jax.random.uniform(jax.random.fold_in(jax.random.fold_in(stream_key, 6), position), (shards_of,), jnp.float32, low / len(cuts), high / len(cuts))
        loudness = loudness * jnp.repeat(jnp.exp(heights), dims[position] // shards_of).reshape((-1,) + (1,) * (len(dims) - 1 - position))
    return loudness


def noise(key, dims, deviation, reach, shards=(), held_as=jnp.bfloat16):
    result = jax.random.normal(key, dims, jnp.float32) * deviation
    if len(shards) > 0:
        result = block_levels(key, dims, shards, -0.22, 0.18) * result
    return jnp.clip(result, min=-reach, max=reach).astype(held_as)


def setup_inputs(seed: int = 0) -> dict:
    key_of = jax.random.split(jax.random.key(seed), 7)
    return {
        "green_blocks": noise(key_of[0], (NK, NE, NC, 2, O, O), 1.0, 6.0, ((0, 4), (1, 2), (2, 4))),
        "coupling": noise(key_of[1], (NQ, NC, NB, O, O), (4 * O) ** -0.5, 0.25, ((1, 4),)),
        "neighbours": draw_neighbours(jax.random.fold_in(key_of[6], 71), 0),
        "momentum_shift": draw_momentum_shift(jax.random.fold_in(key_of[6], 71), 0),
        "energy_offset": draw_energy_offset(jax.random.fold_in(key_of[6], 71), 0),
        "phonon_weight": jnp.clip(jnp.exp(jax.random.uniform(key_of[5], (NW,), jnp.float32, math.log(0.3), math.log(1.5))), 0.3, 1.5),
    }


def reference(green_blocks, coupling, neighbours, momentum_shift, energy_offset, phonon_weight):
    couple = coupling.astype(jnp.float32)
    moment_grid = jnp.repeat(jnp.arange(NK, dtype=jnp.int32), NE)
    energy_grid = jnp.tile(jnp.arange(NE, dtype=jnp.int32), NK)

    def one_point(point_pair):
        moment_now = point_pair[0]
        energy_now = point_pair[1]
        source_rows = ((moment_now - momentum_shift) % NK).astype(jnp.int32)
        chosen = green_blocks[source_rows, energy_now]
        picked = chosen[:, neighbours].astype(jnp.float32)
        left_products = jnp.einsum("tajxy,tajryz->tajrxz", couple, picked).astype(jnp.bfloat16)
        left_products = lax.optimization_barrier(left_products).astype(jnp.float32)
        return jnp.einsum("tajrxz,tajwz->arxw", left_products, couple)

    scattering_terms = lax.map(one_point, (moment_grid, energy_grid))
    scattering_terms = scattering_terms.reshape((NK, NE, NC, 2, O, O))
    padded = jnp.pad(scattering_terms, ((0, 0), (OFFMAX, 0), (0, 0), (0, 0), (0, 0), (0, 0)))
    self_energy = jnp.zeros((NK, NE, NC, 2, O, O), jnp.float32)
    for phonon in range(NW):
        start_row = (OFFMAX - energy_offset[phonon]).astype(jnp.int32)
        shifted = lax.dynamic_slice_in_dim(padded, start_row, NE, axis=1)
        self_energy = self_energy + phonon_weight[phonon] * shifted
    return self_energy
```

```python
import functools

import jax
import jax.numpy as jnp
from jax import lax
from jax.experimental import pallas as pl
from jax.experimental.pallas import tpu as pltpu
from jax.sharding import PartitionSpec as P

REACH = 2
OFFMAX = 2
MESH = pl.DeviceIdType.MESH
PAIR = 2


def kernel(dims, counts, *refs):
    mom_local, energy_local, cluster_local, parts, size, branches, bonds, phonons = dims
    mom_count, en_count, atom_count = counts
    green, coupling, neighbours, shift, offset, weight, out = refs[:7]
    ext = refs[7 : 7 + energy_local]
    (
        couple, couple_t, left, terms, upper, lower, stage,
        own_sem, load_sem, send_sem, recv_sem, up_send, up_recv, out_sem,
    ) = refs[7 + energy_local :]
    pairs = branches * bonds
    mom = lax.axis_index("mom")
    en = lax.axis_index("en")
    atom = lax.axis_index("atom")
    mom_next = {"mom": lax.rem(mom + 1, mom_count)}
    mom_prev = {"mom": lax.rem(mom + mom_count - 1, mom_count)}
    atom_next = {"atom": lax.rem(atom + 1, atom_count)}
    atom_prev = {"atom": lax.rem(atom + atom_count - 1, atom_count)}
    en_next = {"en": lax.rem(en + 1, en_count)}
    en_prev = {"en": lax.rem(en + en_count - 1, en_count)}

    barrier = pltpu.get_barrier_semaphore()
    for device in (mom_next, mom_prev, atom_next, atom_prev, en_next, en_prev):
        pl.semaphore_signal(barrier, inc=1, device_id=device, device_id_type=MESH)
    pl.semaphore_wait(barrier, 6)

    def remote(e, slot, source, target, device):
        return pltpu.make_async_remote_copy(
            src_ref=source,
            dst_ref=target,
            send_sem=send_sem.at[e, slot],
            recv_sem=recv_sem.at[e, slot],
            device_id=device,
            device_id_type=MESH,
        )

    low = pl.ds(0, REACH)
    mid_k = pl.ds(REACH, mom_local)
    mid_a = pl.ds(REACH, cluster_local)
    high_k = pl.ds(REACH + mom_local, REACH)
    high_a = pl.ds(REACH + cluster_local, REACH)
    last_a = pl.ds(cluster_local, REACH)
    first_a = pl.ds(REACH, REACH)

    own = [
        pltpu.make_async_copy(green.at[:, e], ext[e].at[mid_k, mid_a], own_sem.at[e])
        for e in range(energy_local)
    ]
    mom_copies = [
        (
            remote(e, 0, green.at[pl.ds(mom_local - REACH, REACH), e], ext[e].at[low, mid_a], mom_next),
            remote(e, 1, green.at[low, e], ext[e].at[high_k, mid_a], mom_prev),
        )
        for e in range(energy_local)
    ]
    atom_copies = [
        (
            remote(e, 2, green.at[:, e, pl.ds(cluster_local - REACH, REACH)], ext[e].at[mid_k, low], atom_next),
            remote(e, 3, green.at[:, e, low], ext[e].at[mid_k, high_a], atom_prev),
        )
        for e in range(energy_local)
    ]
    corner_copies = [
        (
            remote(e, 4, ext[e].at[low, last_a], ext[e].at[low, low], atom_next),
            remote(e, 5, ext[e].at[low, first_a], ext[e].at[low, high_a], atom_prev),
            remote(e, 6, ext[e].at[high_k, last_a], ext[e].at[high_k, low], atom_next),
            remote(e, 7, ext[e].at[high_k, first_a], ext[e].at[high_k, high_a], atom_prev),
        )
        for e in range(energy_local)
    ]
    up_copies = [
        pltpu.make_async_remote_copy(
            src_ref=upper.at[i],
            dst_ref=lower.at[i],
            send_sem=up_send.at[i],
            recv_sem=up_recv.at[i],
            device_id=en_next,
            device_id_type=MESH,
        )
        for i in range(OFFMAX)
    ]
    out_copies = [None] * energy_local

    order = list(range(energy_local - OFFMAX, energy_local)) + list(range(energy_local - OFFMAX))
    for e in order:
        for copy in mom_copies[e]:
            copy.start()
        if e == order[0]:
            for copy in atom_copies[e]:
                copy.start()
    load = pltpu.make_async_copy(coupling, couple, load_sem)
    load.start()
    for e in order:
        own[e].start()
    for copy in atom_copies[order[1]]:
        copy.start()
    load.wait()

    def transpose_one(index, carry):
        a = index // pairs
        p = index % pairs
        row = pl.multiple_of(p * size, size)
        couple_t[a, pl.ds(row, size), :] = couple[p // bonds, a, p % bonds].T
        return carry

    lax.fori_loop(0, cluster_local * pairs, transpose_one, 0)

    mix = []
    for distance in range(1, OFFMAX + 1):
        total = jnp.float32(0.0)
        for w in range(phonons):
            total = total + jnp.where(offset[w] == distance, weight[w], jnp.float32(0.0))
        mix.append(total)
    keep = jnp.where(en > 0, jnp.float32(1.0), jnp.float32(0.0))
    clusters = cluster_local * atom_count
    groups = mom_local // PAIR

    def compute(e):
        def one(index, carry):
            a = index // groups
            k0 = (index % groups) * PAIR
            cluster = atom * cluster_local + a
            nears = [
                jnp.minimum(
                    lax.rem(neighbours[a * bonds + j] - cluster + REACH + clusters, clusters), 2 * REACH
                )
                + a
                for j in range(bonds)
            ]
            for p in range(pairs):
                t, j = divmod(p, bonds)
                near = nears[j]
                for step in range(PAIR):
                    block = ext[e][k0 + step + REACH - shift[t], near]
                    both = jnp.concatenate([block[0], block[1]], axis=1)
                    product = jnp.dot(
                        couple[t, a, j], both, preferred_element_type=jnp.float32
                    ).astype(jnp.bfloat16)
                    for part in range(parts):
                        left[pl.ds((step * parts + part) * size, size), pl.ds(p * size, size)] = product[
                            :, part * size : (part + 1) * size
                        ]
            result = jnp.dot(left[...], couple_t[a], preferred_element_type=jnp.float32)
            result = result.reshape(PAIR, parts, size, size)
            for step in range(PAIR):
                terms[e, k0 + step, a] = result[step]
                if e >= energy_local - OFFMAX:
                    upper[e - (energy_local - OFFMAX), k0 + step, a] = result[step].astype(jnp.bfloat16)
            return carry

        lax.fori_loop(0, cluster_local * groups, one, 0)

    started = []

    def emit(e):
        if len(started) >= 2:
            out_copies[started[-2]].wait()
        slot = len(started) % 2
        started.append(e)
        out_copies[e] = pltpu.make_async_copy(stage.at[slot], out.at[:, e], out_sem.at[e])

        def source(distance, k, a):
            if e - distance >= 0:
                return terms[e - distance, k, a] * mix[distance - 1]
            return lower[OFFMAX + e - distance, k, a].astype(jnp.float32) * (keep * mix[distance - 1])

        def one(index, carry):
            k = index // cluster_local
            a = index % cluster_local
            total = source(1, k, a)
            for distance in range(2, OFFMAX + 1):
                total = total + source(distance, k, a)
            stage[slot, k, a] = total
            return carry

        lax.fori_loop(0, mom_local * cluster_local, one, 0)
        out_copies[e].start()

    def finish(i):
        e = order[i]
        own[e].wait()
        for copy in atom_copies[e] + corner_copies[e]:
            copy.wait_recv()
        compute(e)

    done = set()

    def emit_ready(through):
        have = set(order[: through + 1])
        for e in range(OFFMAX, energy_local):
            if e not in done and all(e - d in have for d in range(1, OFFMAX + 1)):
                done.add(e)
                emit(e)

    for i, e in enumerate(order):
        for copy in mom_copies[e]:
            copy.wait_recv()
        for copy in corner_copies[e]:
            copy.start()
        if i + 2 < energy_local:
            for copy in atom_copies[order[i + 2]]:
                copy.start()
        if 2 <= i < 2 + OFFMAX:
            up_copies[i - 2].start()
        if i >= 1:
            finish(i - 1)
            emit_ready(i - 1)
    for copy in up_copies:
        copy.wait_recv()
    for e in range(OFFMAX):
        emit(e)
    finish(energy_local - 1)
    emit_ready(energy_local - 1)
    for e in started[-2:]:
        out_copies[e].wait()
    for e in range(energy_local):
        for copy in mom_copies[e] + atom_copies[e] + corner_copies[e]:
            copy.wait_send()
    for copy in up_copies:
        copy.wait_send()


def per_device(green, coupling, neighbours, shift, offset, weight):
    mom_local, energy_local, cluster_local, parts, size, _ = green.shape
    branches, _, bonds = coupling.shape[:3]
    phonons = offset.shape[0]
    pairs = branches * bonds
    counts = tuple(lax.axis_size(name) for name in ("mom", "en", "atom"))
    dims = (mom_local, energy_local, cluster_local, parts, size, branches, bonds, phonons)
    extended = (mom_local + 2 * REACH, cluster_local + 2 * REACH, parts, size, size)
    block = (mom_local, cluster_local, parts, size, size)
    smem = pl.BlockSpec(memory_space=pltpu.SMEM)
    hbm = pl.BlockSpec(memory_space=pl.ANY)
    dma = pltpu.SemaphoreType.DMA
    return pl.pallas_call(
        functools.partial(kernel, dims, counts),
        out_shape=jax.ShapeDtypeStruct(green.shape, jnp.float32),
        in_specs=[hbm, hbm, smem, smem, smem, smem],
        out_specs=hbm,
        scratch_shapes=[pltpu.VMEM(extended, jnp.bfloat16) for _ in range(energy_local)]
        + [
            pltpu.VMEM(coupling.shape, jnp.bfloat16),
            pltpu.VMEM((cluster_local, pairs * size, size), jnp.bfloat16),
            pltpu.VMEM((PAIR * parts * size, pairs * size), jnp.bfloat16),
            pltpu.VMEM((energy_local,) + block, jnp.float32),
            pltpu.VMEM((OFFMAX,) + block, jnp.bfloat16),
            pltpu.VMEM((OFFMAX,) + block, jnp.bfloat16),
            pltpu.VMEM((2,) + block, jnp.float32),
            dma((energy_local,)),
            dma,
            dma((energy_local, 8)),
            dma((energy_local, 8)),
            dma((OFFMAX,)),
            dma((OFFMAX,)),
            dma((energy_local,)),
        ],
        compiler_params=pltpu.CompilerParams(
            collective_id=0, has_side_effects=True, vmem_limit_bytes=67043328
        ),
    )(green, coupling, neighbours.reshape(-1), shift, offset, weight)


def solution(mesh):
    return jax.shard_map(
        per_device,
        mesh=mesh,
        in_specs=(
            P("mom", "en", "atom", None, None, None),
            P(None, "atom", None, None, None),
            P("atom", None),
            P(),
            P(),
            P(),
        ),
        out_specs=P("mom", "en", "atom", None, None, None),
        check_vma=False,
    )
```

```python
import functools

import jax
import jax.numpy as jnp
from jax import lax
from jax.experimental import pallas as pl
from jax.experimental.pallas import tpu as pltpu
from jax.sharding import PartitionSpec as P

REACH = 2
OFFMAX = 2
MESH = pl.DeviceIdType.MESH
PAIR = 2


def kernel(dims, counts, *refs):
    mom_local, energy_local, cluster_local, parts, size, branches, bonds, phonons = dims
    mom_count, en_count, atom_count = counts
    units = energy_local * parts
    kept = parts // 2
    top = energy_local - 1
    green, coupling, neighbours, shift, offset, weight, out = refs[:7]
    ext = refs[7 : 7 + units]
    (
        couple, couple_t, left, terms, upper, lower, stage,
        own_sem, load_sem, send_sem, recv_sem, up_send, up_recv, pass_send, pass_recv, out_sem,
    ) = refs[7 + units :]
    pairs = branches * bonds
    mom = lax.axis_index("mom")
    en = lax.axis_index("en")
    atom = lax.axis_index("atom")
    mom_next = {"mom": lax.rem(mom + 1, mom_count)}
    mom_prev = {"mom": lax.rem(mom + mom_count - 1, mom_count)}
    atom_next = {"atom": lax.rem(atom + 1, atom_count)}
    atom_prev = {"atom": lax.rem(atom + atom_count - 1, atom_count)}
    en_next = {"en": lax.rem(en + 1, en_count)}
    en_prev = {"en": lax.rem(en + en_count - 1, en_count)}
    has_next = en < en_count - 1
    has_prev = en > 0

    barrier = pltpu.get_barrier_semaphore()
    for device in (mom_next, mom_prev, atom_next, atom_prev, en_next, en_prev):
        pl.semaphore_signal(barrier, inc=1, device_id=device, device_id_type=MESH)
    pl.semaphore_wait(barrier, 6)

    low = pl.ds(0, REACH)
    mid_k = pl.ds(REACH, mom_local)
    mid_a = pl.ds(REACH, cluster_local)
    high_k = pl.ds(REACH + mom_local, REACH)
    high_a = pl.ds(REACH + cluster_local, REACH)
    last_k = pl.ds(mom_local, REACH)
    last_a = pl.ds(cluster_local, REACH)
    first = pl.ds(REACH, REACH)
    tail_k = pl.ds(mom_local - REACH, REACH)
    tail_a = pl.ds(cluster_local - REACH, REACH)

    def energy_part(u):
        return divmod(u, parts)

    def guarded(u, body):
        e, part = energy_part(u)
        if e < top:
            body()
        elif part < kept:
            pl.when(has_next)(body)
        else:
            pl.when(has_prev)(body)

    def passed(u):
        e, part = energy_part(u)
        return e == top and part >= kept

    def remote(u, slot, source, target, device):
        return pltpu.make_async_remote_copy(
            src_ref=source,
            dst_ref=target,
            send_sem=send_sem.at[u, slot],
            recv_sem=recv_sem.at[u, slot],
            device_id=device,
            device_id_type=MESH,
        )

    def own_copy(u):
        e, part = energy_part(u)
        return pltpu.make_async_copy(green.at[:, e, :, part], ext[u].at[mid_k, mid_a], own_sem.at[u])

    def pass_copy(u):
        e, part = energy_part(u)
        return pltpu.make_async_remote_copy(
            src_ref=green.at[:, e, :, part],
            dst_ref=ext[u].at[mid_k, mid_a],
            send_sem=pass_send.at[part - kept],
            recv_sem=pass_recv.at[part - kept],
            device_id=en_next,
            device_id_type=MESH,
        )

    def mom_copies(u):
        e, part = energy_part(u)
        if passed(u):
            tail, head = ext[u].at[last_k, mid_a], ext[u].at[first, mid_a]
        else:
            tail, head = green.at[tail_k, e, :, part], green.at[low, e, :, part]
        return (
            remote(u, 0, tail, ext[u].at[low, mid_a], mom_next),
            remote(u, 1, head, ext[u].at[high_k, mid_a], mom_prev),
        )

    def atom_copies(u):
        e, part = energy_part(u)
        if passed(u):
            tail, head = ext[u].at[mid_k, last_a], ext[u].at[mid_k, first]
        else:
            tail, head = green.at[:, e, tail_a, part], green.at[:, e, low, part]
        return (
            remote(u, 2, tail, ext[u].at[mid_k, low], atom_next),
            remote(u, 3, head, ext[u].at[mid_k, high_a], atom_prev),
        )

    def corner_copies(u):
        return (
            remote(u, 4, ext[u].at[low, last_a], ext[u].at[low, low], atom_next),
            remote(u, 5, ext[u].at[low, first], ext[u].at[low, high_a], atom_prev),
            remote(u, 6, ext[u].at[high_k, last_a], ext[u].at[high_k, low], atom_next),
            remote(u, 7, ext[u].at[high_k, first], ext[u].at[high_k, high_a], atom_prev),
        )

    def start(copies):
        for copy in copies:
            copy.start()

    def wait_recv(copies):
        for copy in copies:
            copy.wait_recv()

    def up_copy(i):
        return pltpu.make_async_remote_copy(
            src_ref=upper.at[i],
            dst_ref=lower.at[i],
            send_sem=up_send.at[i],
            recv_sem=up_recv.at[i],
            device_id=en_next,
            device_id_type=MESH,
        )

    whole = [(top - 1) * parts + part for part in range(parts)]
    stay = [top * parts + part for part in range(kept)]
    moved = [top * parts + part for part in range(kept, parts)]
    others = list(range((top - 1) * parts))
    order = whole + stay + others[:parts] + moved + others[parts:]
    messages = whole + stay
    ahead = 4

    def start_moms(u):
        def body():
            if passed(u):
                pass_copy(u).wait_recv()
            start(mom_copies(u))

        guarded(u, body)

    for u in order[:2]:
        start_moms(u)
    for u in moved:
        pl.when(has_next)(lambda u=u: pass_copy(u).start())
    guarded(order[0], lambda: start(atom_copies(order[0])))
    for u in order[2:ahead]:
        start_moms(u)
    load = pltpu.make_async_copy(coupling, couple, load_sem)
    load.start()
    for u in order:
        if not passed(u):
            guarded(u, lambda u=u: own_copy(u).start())
    guarded(order[1], lambda: start(atom_copies(order[1])))
    load.wait()

    def transpose_one(index, carry):
        a = index // pairs
        p = index % pairs
        row = pl.multiple_of(p * size, size)
        couple_t[a, pl.ds(row, size), :] = couple[p // bonds, a, p % bonds].T
        return carry

    lax.fori_loop(0, cluster_local * pairs, transpose_one, 0)

    @pl.when(jnp.logical_not(has_prev))
    def _():
        def clear(index, carry):
            k = index // cluster_local
            a = index % cluster_local
            for i in range(len(messages)):
                lower[i, k, a] = jnp.zeros((size, size), jnp.bfloat16)
            for part in range(kept, parts):
                terms[0, part, k, a] = jnp.zeros((size, size), jnp.float32)
            return carry

        lax.fori_loop(0, mom_local * cluster_local, clear, 0)

    mix = []
    for distance in range(1, OFFMAX + 1):
        total = jnp.float32(0.0)
        for w in range(phonons):
            total = total + jnp.where(offset[w] == distance, weight[w], jnp.float32(0.0))
        mix.append(total)
    clusters = cluster_local * atom_count
    groups = mom_local // PAIR

    def compute(u):
        e, part = energy_part(u)

        def one(index, carry):
            a = index // groups
            k0 = (index % groups) * PAIR
            cluster = atom * cluster_local + a
            nears = [
                jnp.minimum(
                    lax.rem(neighbours[a * bonds + j] - cluster + REACH + clusters, clusters), 2 * REACH
                )
                + a
                for j in range(bonds)
            ]
            for p in range(pairs):
                t, j = divmod(p, bonds)
                row = k0 + REACH - shift[t]
                both = jnp.concatenate([ext[u][row + step, nears[j]] for step in range(PAIR)], axis=1)
                product = jnp.dot(
                    couple[t, a, j], both, preferred_element_type=jnp.float32
                ).astype(jnp.bfloat16)
                for step in range(PAIR):
                    left[pl.ds(step * size, size), pl.ds(p * size, size)] = product[
                        :, step * size : (step + 1) * size
                    ]
            result = jnp.dot(left[...], couple_t[a], preferred_element_type=jnp.float32)
            for step in range(PAIR):
                block = result[step * size : (step + 1) * size]
                if e < top:
                    terms[e + 1, part, k0 + step, a] = block
                elif part >= kept:
                    terms[0, part, k0 + step, a] = block
                if u in messages:
                    upper[messages.index(u), k0 + step, a] = block.astype(jnp.bfloat16)
            return carry

        lax.fori_loop(0, cluster_local * groups, one, 0)

    started = []

    def out_copy(slot, e, part):
        return pltpu.make_async_copy(stage.at[slot], out.at[:, e, :, part], out_sem.at[slot])

    def emit(e, part):
        slot = len(started) % 2
        if len(started) >= 2:
            out_copy(slot, *started[-2]).wait()
        started.append((e, part))

        def source(before, k, a):
            if before >= 0:
                return terms[before + 1, part, k, a]
            if before == -1:
                if part >= kept:
                    return terms[0, part, k, a]
                return lower[parts + part, k, a].astype(jnp.float32)
            return lower[part, k, a].astype(jnp.float32)

        def one(index, carry):
            k = index // cluster_local
            a = index % cluster_local
            total = source(e - 1, k, a) * mix[0]
            for distance in range(2, OFFMAX + 1):
                total = total + source(e - distance, k, a) * mix[distance - 1]
            stage[slot, k, a] = total
            return carry

        lax.fori_loop(0, mom_local * cluster_local, one, 0)
        out_copy(slot, e, part).start()

    def finish(i):
        u = order[i]

        def body():
            if not passed(u):
                own_copy(u).wait()
            wait_recv(atom_copies(u) + corner_copies(u))
            compute(u)

        guarded(u, body)

    done = set()

    def emit_ready(through):
        have = set(order[: through + 1])
        for e in range(OFFMAX, energy_local):
            for part in range(parts):
                if (e, part) not in done and all(
                    (e - d) * parts + part in have for d in range(1, OFFMAX + 1)
                ):
                    done.add((e, part))
                    emit(e, part)

    for i, u in enumerate(order):

        def step(u=u):
            wait_recv(mom_copies(u))
            start(corner_copies(u))

        guarded(u, step)
        if i + ahead < units:
            start_moms(order[i + ahead])
        if i + 2 < units:
            guarded(order[i + 2], lambda v=order[i + 2]: start(atom_copies(v)))
        if 2 <= i < 2 + len(messages):
            pl.when(has_next)(lambda i=i: up_copy(i - 2).start())
        if i >= 1:
            finish(i - 1)
            emit_ready(i - 1)
        if i == units - 2:

            @pl.when(has_prev)
            def _():
                for n in range(len(messages)):
                    up_copy(n).wait_recv()

            for e in range(OFFMAX):
                for part in range(parts):
                    emit(e, part)
    finish(units - 1)
    emit_ready(units - 1)
    for n in (2, 1):
        out_copy((len(started) - n) % 2, *started[-n]).wait()
    for u in order:

        def drain(u=u):
            for copy in mom_copies(u) + atom_copies(u) + corner_copies(u):
                copy.wait_send()

        guarded(u, drain)

    @pl.when(has_next)
    def _():
        for n in range(len(messages)):
            up_copy(n).wait_send()
        for u in moved:
            pass_copy(u).wait_send()


def per_device(green, coupling, neighbours, shift, offset, weight):
    mom_local, energy_local, cluster_local, parts, size, _ = green.shape
    branches, _, bonds = coupling.shape[:3]
    phonons = offset.shape[0]
    pairs = branches * bonds
    counts = tuple(lax.axis_size(name) for name in ("mom", "en", "atom"))
    dims = (mom_local, energy_local, cluster_local, parts, size, branches, bonds, phonons)
    extended = (mom_local + 2 * REACH, cluster_local + 2 * REACH, size, size)
    block = (mom_local, cluster_local, size, size)
    units = energy_local * parts
    sent = parts + parts // 2
    smem = pl.BlockSpec(memory_space=pltpu.SMEM)
    hbm = pl.BlockSpec(memory_space=pl.ANY)
    dma = pltpu.SemaphoreType.DMA
    return pl.pallas_call(
        functools.partial(kernel, dims, counts),
        out_shape=jax.ShapeDtypeStruct(green.shape, jnp.float32),
        in_specs=[hbm, hbm, smem, smem, smem, smem],
        out_specs=hbm,
        scratch_shapes=[pltpu.VMEM(extended, jnp.bfloat16) for _ in range(units)]
        + [
            pltpu.VMEM(coupling.shape, jnp.bfloat16),
            pltpu.VMEM((cluster_local, pairs * size, size), jnp.bfloat16),
            pltpu.VMEM((PAIR * size, pairs * size), jnp.bfloat16),
            pltpu.VMEM((energy_local, parts) + block, jnp.float32),
            pltpu.VMEM((sent,) + block, jnp.bfloat16),
            pltpu.VMEM((sent,) + block, jnp.bfloat16),
            pltpu.VMEM((2,) + block, jnp.float32),
            dma((units,)),
            dma,
            dma((units, 8)),
            dma((units, 8)),
            dma((sent,)),
            dma((sent,)),
            dma((parts - parts // 2,)),
            dma((parts - parts // 2,)),
            dma((2,)),
        ],
        compiler_params=pltpu.CompilerParams(
            collective_id=0, has_side_effects=True, vmem_limit_bytes=67043328
        ),
    )(green, coupling, neighbours.reshape(-1), shift, offset, weight)


def solution(mesh):
    return jax.shard_map(
        per_device,
        mesh=mesh,
        in_specs=(
            P("mom", "en", "atom", None, None, None),
            P(None, "atom", None, None, None),
            P("atom", None),
            P(),
            P(),
            P(),
        ),
        out_specs=P("mom", "en", "atom", None, None, None),
        check_vma=False,
    )
```
